512 devices in a mesh: src: 64 (over x, y, core), inst: 8 (over z).
Axes of the slice: x: 4, y: 8, z: 8, core: 2. Of those that a mesh axis runs over, the one named last changes fastest.
Arguments:
- observed: float32 [60, 262144], P(None, ('src', 'inst')), may hold values from -18 to 18
- basis: float32 [60, 55], replicated, may hold values from -0.875 to 0.875
- taps: float32 [9], replicated, may hold values from 0.05 to 0.35
- epoch_owner: int32 [262144, 1], P(('src', 'inst')), may hold values from 0 to 63; in each aligned block of 512 rows (0 to 511, 512 to 1023, ...) at most 12 rows name the same one
- epoch_source: int32 [262144], P(('src', 'inst')), may hold values from 0 to 4095
- epoch_config: int32 [262144], P(('src', 'inst')), may hold values from 0 to 127
- epoch_counts: int32 [512], P(('src', 'inst')), may hold values from 256 to 512, as said below
Outputs:
- solution_coeffs: float32 [55, 262144], P(None, 'src')
- solution_table: float32 [60, 128], P(None, 'inst')
- direction_coeffs: float32 [55, 262144], P(None, 'src')
- direction_table: float32 [60, 128], P(None, 'inst')
The draws below stay inside these ranges and needn't reach their ends.
Inputs may be any that keep to these rules, and one draw needn't show every extreme that they name: `epoch_owner`: among the 512 epochs of one device, at most 12 name any one owner. The first epoch_counts[d] of device d's 512 epoch slots are live.
All inputs are finite; a program needn't handle non-finite values.
Results may differ from the reference program's by a relative error of at most 0.0003.
Values sent between devices are 32-bit elements; how exact they have to be, the bound alone decides.
No kernel may reach another device: no remote copies, remote signals or barrier semaphores. Data moves between devices by JAX's collectives and lax.ppermute only.
A program may use at most 64 MiB of HBM per device.

```python
import math
import jax
import jax.numpy as jnp
import numpy as np
from jax import lax

SAMPLES = 60
NCOEF = 55
TAPS = 9
ITERS = 2
EPD = 512
SRC_DEV = 4096
CAP = 12
SHARDS = 512
EPOCHS = 262144
SOURCES = 262144
CONFIGS = 128
N_SRC = 64


def draw_observed(key, part):
    cols = jnp.arange(EPOCHS, dtype=jnp.float32)
    rising = 1.0 + 2.0 * cols / EPOCHS
    values = jnp.clip(jax.random.normal(key, (SAMPLES, EPOCHS), jnp.float32), -6.0, 6.0)
    return values * rising[None, :]


def draw_epoch_counts(key, part):
    first, second = jax.random.split(key, 2)
    base = jax.random.randint(first, (SHARDS,), EPD // 2, EPD + 1)
    fullest = jax.random.randint(second, (), 0, SHARDS)
    return jnp.where(jnp.arange(SHARDS) == fullest, EPD, base).astype(jnp.int32)


def set_ends(array, own_key, smallest, high):
    index_at = [jax.random.randint(jax.random.fold_in(own_key, axis), (), 0, length) for axis, length in enumerate(array.shape)]
    longest = array.shape.index(max(array.shape))
    neighbour = index_at[:longest] + [(index_at[longest] + 1) % array.shape[longest]] + index_at[longest + 1:]
    return array.at[tuple(index_at)].set(smallest).at[tuple(neighbour)].set(high)


def assign_block(key, own, number, rows, count, top, most, skew):
    order = jax.random.permutation(key, count)
    crowded, usual = shares(count, rows * top, most, skew, True), shares(count, rows * top, most, skew, False)
    places = jnp.arange(count)

    def named(sizes, rotation):
        used = int((sizes > 0).sum())
        fixed = max(1, used // 4)
        shifted = fixed + (places - fixed + rotation * (used - fixed)) % max(1, count - fixed)
        return jnp.zeros((count,), jnp.int32).at[order[jnp.where(places < fixed, places, shifted)]].set(jnp.asarray(sizes, jnp.int32))

    sizes = jnp.where(number % 4 == 0, named(crowded, number // 4), named(usual, number - number // 4 - 1))
    mixed = jax.random.permutation(jax.random.fold_in(own, 3), count)
    donor, sink = mixed[0:count // 2 * 2:2], mixed[1:count // 2 * 2:2]
    slack = jnp.minimum(sizes[donor] - 1, most - sizes[sink]) // 2
    slack = jnp.where((donor == order[0]) | (sink == order[0]) | (sizes[sink] == 0), 0, jnp.maximum(slack, 0))
    shifted = jax.random.randint(jax.random.fold_in(own, 4), (count // 2,), 0, 1 << 20) % (slack + 1)
    sizes = sizes.at[donor].add(-shifted).at[sink].add(shifted)
    items = jnp.searchsorted(jnp.cumsum(sizes), jnp.arange(rows * top), side="right").astype(jnp.int32)
    listing = items.reshape(top, rows).T
    listing = listing[jax.random.permutation(jax.random.fold_in(own, 1), rows)]
    rotation = jax.random.randint(jax.random.fold_in(own, 2), (rows, 1), 0, top)
    return jnp.take_along_axis(listing, (jnp.arange(top)[None, :] + rotation) % top, axis=1)


def shares(amount, total, limit, skew, full):
    portions = [(1 << 20) // math.isqrt(grade ** skew) + 1 for grade in range(1, amount + 1)]
    largest = limit if full else min(limit, max(-(-total // amount), total * portions[0] // sum(portions)))
    least = 1 if total - largest >= amount - 1 else 0
    holding, spare = [largest] + [least] * (amount - 1), total - largest - least * (amount - 1)
    while spare > 0:
        movable = [i for i in range(1, amount) if holding[i] < largest] or [i for i in range(1, amount) if holding[i] < limit]
        pool, budget = sum([portions[i] for i in movable]), spare
        for i in movable:
            extra = min(limit - holding[i], max(1, budget * portions[i] // pool), spare)
            holding[i] = holding[i] + extra
            spare = spare - extra
    return np.array(holding)


def noise(key, dims, scale, bound, kind=jnp.bfloat16):
    drawn = jax.random.normal(key, dims, jnp.float32) * scale
    return jnp.minimum(jnp.maximum(drawn, -bound), bound).astype(kind)


def setup_inputs(seed: int = 0) -> dict:
    splits = jax.random.split(jax.random.key(seed), 8)
    observed = draw_observed(jax.random.fold_in(splits[7], 71), 0)
    basis = noise(splits[1], (SAMPLES, NCOEF), NCOEF ** -0.5, 0.875, jnp.float32)
    taps = jnp.clip(jax.random.uniform(splits[2], (TAPS,), jnp.float32, 0.05, 0.35), 0.05, 0.35)
    epoch_owner_keys = jax.random.split(jax.random.fold_in(splits[3], 1), EPOCHS // EPD)
    epoch_owner_turns = jax.random.permutation(jax.random.fold_in(splits[3], 3), EPOCHS // EPD)
    epoch_owner = jax.vmap(lambda own, number: assign_block(jax.random.fold_in(splits[3], 2), own, number, EPD, N_SRC, 1, CAP, 2))(epoch_owner_keys, epoch_owner_turns).reshape((EPOCHS, 1))
    epoch_source = set_ends(jax.random.randint(splits[4], (EPOCHS,), 0, SRC_DEV), jax.random.fold_in(splits[4], 1), 0, SRC_DEV - 1).astype(jnp.int32)
    epoch_config = set_ends(jax.random.randint(splits[5], (EPOCHS,), 0, CONFIGS), jax.random.fold_in(splits[5], 1), 0, CONFIGS - 1).astype(jnp.int32)
    epoch_counts = draw_epoch_counts(jax.random.fold_in(splits[7], 71), 0)
    return dict(observed=observed, basis=basis, taps=taps, epoch_owner=epoch_owner, epoch_source=epoch_source, epoch_config=epoch_config, epoch_counts=epoch_counts)


exact_mode = lax.Precision.HIGHEST

def line_matrix(taps, samples):
    width = taps.shape[0]
    half = width // 2
    rows = lax.broadcasted_iota(jnp.int32, (samples, samples), 0)
    cols = lax.broadcasted_iota(jnp.int32, (samples, samples), 1)
    offset = cols - rows + half
    inside = (offset >= 0) & (offset < width)
    picked = jnp.take(taps, jnp.clip(offset, 0, width - 1))
    return jnp.where(inside, picked, jnp.zeros_like(picked))

def reference(observed, basis, taps, epoch_owner, epoch_source, epoch_config, epoch_counts):
    response = jnp.dot(line_matrix(taps, SAMPLES), basis, precision=exact_mode)
    source_of = (epoch_owner[:, 0] * SRC_DEV + epoch_source).astype(jnp.int32)
    slots = jnp.arange(EPOCHS, dtype=jnp.int32)
    live = (slots % EPD < jnp.repeat(epoch_counts, EPD)).astype(observed.dtype)
    cweight = 0.4 * (1.0 + 3.0 * jnp.arange(CONFIGS, dtype=jnp.int32).astype(observed.dtype) / CONFIGS)

    def forward(coeffs, table):
        model = jnp.dot(response, jnp.take(coeffs, source_of, axis=1), precision=exact_mode)
        model = model + jnp.take(table * cweight[None, :], epoch_config, axis=1)
        return model * live[None, :]

    def adjoint(resid):
        masked = resid * live[None, :]
        terms = jnp.dot(response.T, masked, precision=exact_mode)
        coeffs = jnp.zeros((NCOEF, SOURCES), resid.dtype).at[:, source_of].add(terms)
        table = jnp.zeros((SAMPLES, CONFIGS), resid.dtype).at[:, epoch_config].add(masked)
        return (coeffs, table * cweight[None, :])

    def param_norm(coeffs, table):
        return jnp.sqrt(jnp.sum(coeffs * coeffs) + jnp.sum(table * table))
    resid = observed * live[None, :]
    beta = jnp.sqrt(jnp.sum(resid * resid))
    resid = resid / beta
    dir_c, dir_h = adjoint(resid)
    alpha = param_norm(dir_c, dir_h)
    dir_c = dir_c / alpha
    dir_h = dir_h / alpha
    walk_c, walk_h = (dir_c, dir_h)
    sol_c = jnp.zeros_like(dir_c)
    sol_h = jnp.zeros_like(dir_h)
    phibar = beta
    rhobar = alpha
    for step in range(ITERS):
        resid = forward(dir_c, dir_h) - alpha * resid
        beta = jnp.sqrt(jnp.sum(resid * resid))
        resid = resid / beta
        back_c, back_h = adjoint(resid)
        dir_c = back_c - beta * dir_c
        dir_h = back_h - beta * dir_h
        alpha = param_norm(dir_c, dir_h)
        dir_c = dir_c / alpha
        dir_h = dir_h / alpha
        rho = jnp.sqrt(rhobar * rhobar + beta * beta)
        cosine = rhobar / rho
        sine = beta / rho
        theta = sine * alpha
        rhobar = -cosine * alpha
        phi = cosine * phibar
        phibar = sine * phibar
        sol_c = sol_c + phi / rho * walk_c
        sol_h = sol_h + phi / rho * walk_h
        walk_c = dir_c - theta / rho * walk_c
        walk_h = dir_h - theta / rho * walk_h
    return (sol_c, sol_h, walk_c, walk_h)
```

```python
import functools

import jax
import jax.numpy as jnp
from jax import lax
from jax.experimental import pallas as pl
from jax.experimental.pallas import tpu as pltpu
from jax.sharding import Mesh
from jax.sharding import PartitionSpec as P

ALL = ("x", "y", "c", "z")
SRC = ("x", "y", "c")
PLANE = ("x", "y")
COLUMN = ("c", "z")
SRC_DEV = 4096
CONFIGS = 128
KDEV = 16
SLOTS = 12
ROWS = 64
LOW = 256
HIGH = SRC_DEV // LOW
SIGMA = 2.0**-13
HI = lax.Precision.HIGHEST
F32 = jnp.float32
BF16 = jnp.bfloat16


def iota(shape, dim):
    return lax.broadcasted_iota(jnp.int32, shape, dim)


def nt(a, b, **kw):
    return lax.dot_general(a, b, (((1,), (1,)), ((), ())), preferred_element_type=F32, **kw)


def tn(a, b, **kw):
    return lax.dot_general(a, b, (((0,), (0,)), ((), ())), preferred_element_type=F32, **kw)


def nn(a, b, **kw):
    return lax.dot_general(a, b, (((1,), (0,)), ((), ())), preferred_element_type=F32, **kw)


def thirds(v):
    first = v.astype(BF16)
    rest = v - first.astype(F32)
    second = rest.astype(BF16)
    return first, second, (rest - second.astype(F32)).astype(BF16)


def response_kernel(taps_ref, basis_ref, out_ref):
    samples = basis_ref.shape[0]
    half = taps_ref.shape[0] // 2
    offset = iota((samples, samples), 1) - iota((samples, samples), 0) + half
    lsf = jnp.zeros((samples, samples), F32)
    for t in range(taps_ref.shape[0]):
        lsf = jnp.where(offset == t, taps_ref[t], lsf)
    out_ref[...] = jnp.zeros_like(out_ref)
    out_ref[0:samples, 0 : basis_ref.shape[1]] = nn(lsf, basis_ref[...], precision=HI)


def pack_kernel(counts_ref, obs_ref, owner_ref, source_ref, config_ref, out_ref):
    samples, epochs = obs_ref.shape
    owners = out_ref.shape[0]
    live = iota((1, epochs), 1) < counts_ref[0]
    x = jnp.concatenate([obs_ref[...], jnp.zeros((ROWS - samples, epochs), F32)], axis=0)
    named = (owner_ref[...] == iota((owners, epochs), 0)) & live
    onehot = named.astype(F32)
    owned = onehot.astype(BF16)
    before = (iota((epochs, epochs), 0) < iota((epochs, epochs), 1)).astype(F32).astype(BF16)
    rank = jnp.sum(onehot * nn(owned, before), axis=0, keepdims=True).astype(jnp.int32)
    row = iota((32, epochs), 0)
    wanted_rank = jnp.where(row < SLOTS, row, row - SLOTS)
    value = jnp.where(row < SLOTS, source_ref[...] + 1, config_ref[...]).astype(F32)
    ints = jnp.where((rank == wanted_rank) & (row < 2 * SLOTS), value, 0.0)
    hits = [rank == t for t in range(SLOTS)]
    for j in range(ROWS // 8):
        part = x[8 * j : 8 * j + 8]
        spread = jnp.concatenate([jnp.where(h, part, 0.0) for h in hits] + [ints], axis=0)
        a, b, c = thirds(spread)
        out_ref[:, j, :] = nt(owned, a) + (nt(owned, b) + nt(owned, c))


def build_kernel(recv_ref, counts_ref, sums_ref, pay_ref, flip_ref, acc_ref, cfg_ref):
    flip_ref[...] = recv_ref[...].T
    acc_ref[...] = jnp.zeros_like(acc_ref)
    cfg_ref[...] = jnp.zeros_like(cfg_ref)
    width = recv_ref.shape[0]

    def step(t, square):
        x = flip_ref[pl.ds(pl.multiple_of(t * 8, 8), 8), :]
        source = flip_ref[pl.ds(8 * SLOTS + t, 1), :].astype(jnp.int32) - 1
        config = flip_ref[pl.ds(9 * SLOTS + t, 1), :].astype(jnp.int32)
        config = jnp.where(source < 0, -1, config)
        high = source >> 8
        low = source & (LOW - 1)
        both = jnp.where(source < 0, -1, high * CONFIGS + config)
        lows = (iota((LOW, width), 0) == low).astype(F32).astype(BF16)
        a, b, c = thirds(x)
        parts = jnp.concatenate(
            [a.astype(F32), b.astype(F32), c.astype(F32), jnp.ones((8, width), F32)], axis=0
        )
        row = iota((CONFIGS, width), 0)
        for h in range(HIGH):
            left = jnp.concatenate(
                [
                    (row + h * CONFIGS == both).astype(F32).astype(BF16),
                    jnp.where(high == h, parts, 0.0).astype(BF16),
                ],
                axis=0,
            )
            acc_ref[h] += nt(left, lows)
        cfg_ref[...] += nt(parts.astype(BF16), (row == config).astype(F32).astype(BF16))
        return square + x * x

    square = lax.fori_loop(0, SLOTS, step, jnp.zeros((8, width), F32))
    total = jnp.sum(jnp.sum(square, axis=1, keepdims=True), axis=0, keepdims=True)
    for h in range(HIGH):
        cols = slice(h * LOW, (h + 1) * LOW)
        counts_ref[:, cols] = acc_ref[h, 0:CONFIGS, :]
        sums = acc_ref[h, CONFIGS : CONFIGS + 8, :] + (
            acc_ref[h, CONFIGS + 8 : CONFIGS + 16, :] + acc_ref[h, CONFIGS + 16 : CONFIGS + 24, :]
        )
        for j in range(sums_ref.shape[0]):
            sums_ref[j, :, cols] = sums
    t0 = cfg_ref[0:8, :] + (cfg_ref[8:16, :] + cfg_ref[16:24, :])
    z0 = nt(sums_ref[0], counts_ref[...], precision=HI)
    misc = jnp.concatenate(
        [cfg_ref[24:25, :], jnp.broadcast_to(total, (1, CONFIGS)), jnp.zeros((6, CONFIGS), F32)],
        axis=0,
    )
    pay = jnp.concatenate([t0, z0, misc], axis=0)
    for k in range(pay_ref.shape[0]):
        pay_ref[k] = pay


def add_kernel(in_ref, out_ref):
    total = jnp.sum(in_ref[...], axis=0)
    for k in range(out_ref.shape[0]):
        out_ref[k] = total


def config_weight():
    return 0.4 * (1.0 + 3.0 * iota((1, CONFIGS), 1).astype(F32) / CONFIGS)


def gathered(in_ref, first):
    half = in_ref.shape[0] // 2
    both = in_ref[0:half, first : first + 8, :] + in_ref[half:, first : first + 8, :]
    return both.reshape(half * 8, CONFIGS)


def inner(a, b):
    return jnp.sum(jnp.sum(a * b, axis=1, keepdims=True), axis=0, keepdims=True)


def middle_kernel(
    place_ref, recv_ref, sums_ref, counts_ref, resp_ref, c0_ref, c1_ref, c2_ref, tab_ref, pay_ref, f_ref
):
    weight = config_weight()
    resp = resp_ref[...]
    t0 = gathered(recv_ref, 0)
    z0 = gathered(recv_ref, 8)
    misc = gathered(recv_ref, 16)
    uses = misc[0:1, :]
    total = misc[1:2, :]
    for j in range(1, 8):
        total = total + misc[8 * j + 1 : 8 * j + 2, :]
    scale = 1.0 / jnp.sqrt(total)
    h0 = t0 * weight * scale
    square = nt(resp, resp, precision=HI)
    y0 = nn(square, z0, precision=HI) * scale
    h1 = SIGMA * weight * (y0 + uses * weight * h0)
    counts = counts_ref[...]
    number = jnp.sum(counts, axis=0, keepdims=True)
    b0 = sums_ref[...] * scale[:, 0:1]
    c0 = tn(resp, b0, precision=HI)
    b1 = SIGMA * (number * nn(resp, c0, precision=HI) + nn(h0 * weight, counts, precision=HI))
    c1 = tn(resp, b1, precision=HI)
    f1 = nn(resp, c1, precision=HI)
    b2 = SIGMA * (number * f1 + nn(h1 * weight, counts, precision=HI))
    c2 = tn(resp, b2, precision=HI)
    c0_ref[...] = c0
    c1_ref[...] = c1
    c2_ref[...] = c2
    tab_ref[0] = h0
    tab_ref[1] = h1
    tab_ref[2] = jnp.broadcast_to(uses, h0.shape)
    tab_ref[3] = jnp.broadcast_to(total, h0.shape)
    f_ref[...] = f1
    z1 = nt(f_ref[pl.ds(pl.multiple_of(place_ref[0] * 8, 8), 8), :], counts, precision=HI)
    scalars = [inner(c0, c0), inner(c0, c1), inner(c1, c1), inner(c1, c2), inner(c2, c2)]
    misc = jnp.concatenate(
        [jnp.broadcast_to(s, (1, CONFIGS)) for s in scalars] + [jnp.zeros((3, CONFIGS), F32)], axis=0
    )
    pay = jnp.concatenate([z1, misc], axis=0)
    for k in range(pay_ref.shape[0]):
        pay_ref[k] = pay


def last_kernel(
    place_ref, recv_ref, c0_ref, c1_ref, c2_ref, tab_ref, sol_c_ref, sol_h_ref, dir_c_ref, dir_h_ref
):
    weight = config_weight()
    h0 = tab_ref[0]
    h1 = tab_ref[1]
    uses = tab_ref[2]
    beta1 = jnp.sqrt(tab_ref[3, 0:1, 0:1])
    h2 = SIGMA * weight * (gathered(recv_ref, 0) + uses * weight * h1)
    half = recv_ref.shape[0] // 2
    shared = (recv_ref[0, 8:16, :] + recv_ref[half, 8:16, :])[:, 0:1]
    m0 = shared[0:1] + inner(h0, h0)
    m1 = shared[1:2] + inner(h0, h1)
    m2 = shared[2:3] + inner(h1, h1)
    m3 = shared[3:4] + inner(h1, h2)
    m4 = shared[4:5] + inner(h2, h2)
    alpha1 = jnp.sqrt(m0)
    mu = m1 / m0
    rho1_sq = mu / SIGMA
    rho1 = jnp.sqrt(rho1_sq)
    beta2 = jnp.sqrt(rho1_sq - m0)
    p_sq = m2 - mu * m1
    p = jnp.sqrt(p_sq)
    alpha2 = p / (SIGMA * alpha1 * beta2)
    cs1 = alpha1 / rho1
    sn1 = beta2 / rho1
    theta2 = sn1 * alpha2
    rhobar2 = -cs1 * alpha2
    phi1 = cs1 * beta1
    phibar2 = sn1 * beta1
    q1 = m3 - 2.0 * mu * m2 + mu * mu * m1
    nu = q1 / p_sq
    a2 = nu / SIGMA
    beta3 = jnp.sqrt(a2 - alpha2 * alpha2)
    q_sq = m4 - 2.0 * mu * m3 + mu * mu * m2
    kappa = p_sq / m0
    r = jnp.sqrt(q_sq - nu * q1 - kappa * p_sq)
    alpha3 = r / (SIGMA * p * beta3)
    rho2 = jnp.sqrt(rhobar2 * rhobar2 + beta3 * beta3)
    cs2 = rhobar2 / rho2
    sn2 = beta3 / rho2
    theta3 = sn2 * alpha3
    phi2 = cs2 * phibar2
    tau1 = theta2 / rho1
    tau2 = theta3 / rho2
    w20 = -(mu / p + tau1 / alpha1)
    w21 = 1.0 / p
    step2 = phi2 / rho2
    s0 = phi1 / (rho1 * alpha1) + step2 * w20
    s1 = step2 * w21
    d0 = (mu * nu - kappa) / r - tau2 * w20
    d1 = -(mu + nu) / r - tau2 * w21
    d2 = 1.0 / r
    rows = sol_c_ref.shape[0]
    c0 = c0_ref[0:rows, :]
    c1 = c1_ref[0:rows, :]
    sol_c_ref[...] = s0 * c0 + s1 * c1
    dir_c_ref[...] = d0 * c0 + d1 * c1 + d2 * c2_ref[0:rows, :]
    pick = (iota((CONFIGS, KDEV), 0) == iota((CONFIGS, KDEV), 1) + place_ref[0] * KDEV).astype(F32)
    samples = sol_h_ref.shape[0]
    sol_h_ref[...] = nn(s0 * h0 + s1 * h1, pick, precision=HI)[0:samples]
    dir_h_ref[...] = nn(d0 * h0 + d1 * h1 + d2 * h2, pick, precision=HI)[0:samples]


def vmem():
    return pl.BlockSpec(memory_space=pltpu.VMEM)


def smem():
    return pl.BlockSpec(memory_space=pltpu.SMEM)


def f32(*shape):
    return jax.ShapeDtypeStruct(shape, F32)


def call(kernel, outs, ins, scalars=0, scratch=()):
    return pl.pallas_call(
        kernel,
        out_shape=outs,
        in_specs=[smem()] * scalars + [vmem()] * (len(ins) - scalars),
        out_specs=jax.tree.map(lambda _: vmem(), outs),
        scratch_shapes=list(scratch),
    )(*ins)


def on_device(observed, basis, taps, epoch_owner, epoch_source, epoch_config, epoch_counts):
    owners = lax.axis_size(SRC)
    insts = lax.axis_size("z")
    devices = owners * insts
    plane = lax.axis_size(PLANE)
    column = lax.axis_size(COLUMN)
    samples, epochs = observed.shape
    coeffs = basis.shape[1]
    place = lax.axis_index("z").astype(jnp.int32).reshape(1)
    resp = call(response_kernel, f32(ROWS, ROWS), [taps, basis], 1)
    sent = call(
        pack_kernel,
        f32(owners, insts, 128),
        [
            epoch_counts,
            observed,
            epoch_owner.reshape(1, epochs),
            epoch_source.reshape(1, epochs),
            epoch_config.reshape(1, epochs),
        ],
        1,
    )
    recv = lax.all_to_all(sent.reshape(devices, 1, 128), ALL, 0, 0, tiled=True)
    counts, sums, pay = call(
        build_kernel,
        (f32(CONFIGS, SRC_DEV), f32(insts, 8, SRC_DEV), f32(plane, 24, CONFIGS)),
        [recv.reshape(devices, 128)],
        scratch=[
            pltpu.VMEM((128, devices), F32),
            pltpu.VMEM((HIGH, CONFIGS + 32, LOW), F32),
            pltpu.VMEM((32, CONFIGS), F32),
        ],
    )
    pay = lax.all_to_all(pay, PLANE, 0, 0, tiled=True)
    sums = lax.all_to_all(sums, "z", 0, 0, tiled=True).reshape(ROWS, SRC_DEV)
    pay = call(add_kernel, f32(column, 24, CONFIGS), [pay])
    pay = lax.all_to_all(pay, COLUMN, 0, 0, tiled=True)
    c0, c1, c2, tables, pay = call(
        middle_kernel,
        (
            f32(ROWS, SRC_DEV),
            f32(ROWS, SRC_DEV),
            f32(ROWS, SRC_DEV),
            f32(4, ROWS, CONFIGS),
            f32(plane, 16, CONFIGS),
        ),
        [place, pay, sums, counts, resp],
        1,
        [pltpu.VMEM((ROWS, SRC_DEV), F32)],
    )
    pay = lax.all_to_all(pay, PLANE, 0, 0, tiled=True)
    pay = call(add_kernel, f32(column, 16, CONFIGS), [pay])
    pay = lax.all_to_all(pay, COLUMN, 0, 0, tiled=True)
    return call(
        last_kernel,
        (f32(coeffs, SRC_DEV), f32(samples, KDEV), f32(coeffs, SRC_DEV), f32(samples, KDEV)),
        [place, pay, c0, c1, c2, tables],
        1,
    )


def solution(mesh):
    torus = Mesh(mesh.devices.reshape(4, 8, 2, mesh.shape["inst"]), ALL)
    in_specs = (P(None, ALL), P(), P(), P(ALL, None), P(ALL), P(ALL), P(ALL))
    out_specs = (P(None, SRC), P(None, "z"), P(None, SRC), P(None, "z"))
    return jax.shard_map(
        on_device, mesh=torus, in_specs=in_specs, out_specs=out_specs, check_vma=False
    )
```
